256 devices in a mesh: blk: 8 (over y, core), sep: 32 (over x, z).
Axes of the slice: x: 4, y: 4, z: 8, core: 2. Of those that a mesh axis runs over, the one named last changes fastest.
Arguments:
- interior_inverse: float32 [8, 32, 1024, 1024], P('blk', 'sep'), as said below
- coupling: float32 [8, 32, 1024, 512], P('blk', 'sep')
- port_matrix: float32 [8, 32, 512, 512], P('blk', 'sep'), as said below
- interior_current: float32 [8, 32, 1024, 128], P('blk', 'sep'), may hold values from -6 to 6
- port_current: float32 [8, 32, 512, 128], P('blk', 'sep'), may hold values from -6 to 6
- port_list: int32 [8, 32, 512], P('blk', 'sep'), may hold values from 0 to 1023, as said below
- spectral_scale: float32 [], replicated, may hold values from 1.5 to 3
Outputs:
- port_voltage: float32 [32, 1024, 128], P('sep', 'blk')
- interior_voltage: float32 [8, 32, 1024, 128], P('blk', 'sep')
The draws below stay inside these ranges and needn't reach their ends.
Inputs may be any that keep to these rules, and one draw needn't show every extreme that they name: `port_list`: in each block the first 256 entries are distinct, and so are the last ones. Within one separator group, blocks whose b differ by a multiple of 4 name the same sets, and the sets of the first 4 blocks partition the separator's rows, both for the first and for the last halves. `interior_inverse`: symmetric positive definite. Each block's port_matrix minus coupling^T interior_inverse coupling is symmetric positive definite.
All inputs are finite; a program needn't handle non-finite values.
Results may differ from the reference program's by a relative error of at most 0.0001.
Values sent between devices are 32-bit elements; how exact they have to be, the bound alone decides.
No kernel may reach another device: no remote copies, remote signals or barrier semaphores. Data moves between devices by JAX's collectives and lax.ppermute only.
A program may use at most 64 MiB of HBM per device.

```python
import jax
import jax.numpy as jnp
from jax import lax

NI = 1024
PORTS = 512
NT = 128
SEP_PORTS = 1024
ITERS = 2
DEGREE = 2
N_BLK = 8
N_SEP = 32


HI = lax.Precision.HIGHEST


def block_factors(key, index):
    base = jax.random.fold_in(jax.random.fold_in(key, 5), index)
    first = jax.random.normal(jax.random.fold_in(base, 1), (NI, NI), jnp.float32)
    coupled = jax.random.normal(jax.random.fold_in(base, 2), (NI, PORTS), jnp.float32)
    extra = jax.random.normal(jax.random.fold_in(base, 3), (PORTS, PORTS), jnp.float32)
    inner_shift = jax.random.uniform(jax.random.fold_in(base, 4), (NI,), jnp.float32, 0.5, 2.0)
    port_shift = jax.random.uniform(jax.random.fold_in(base, 5), (PORTS,), jnp.float32, 0.5, 2.0)
    inverse = jnp.dot(first, first.T, precision=HI) / NI + jnp.diag(inner_shift)
    return (inverse, coupled, extra, port_shift)


def largest_value(matrix):

    def turn(vector, unused):
        image = jnp.dot(matrix, vector, precision=HI)
        return (image / jnp.sqrt(jnp.sum(image * image)), None)
    start = jnp.ones((matrix.shape[0],), jnp.float32) / jnp.sqrt(matrix.shape[0] * 1.0)
    vector, unused = lax.scan(turn, start, None, length=40)
    return jnp.sum(vector * jnp.dot(matrix, vector, precision=HI))


def draw_interior_inverse(key, part):

    def single(index):
        inverse, coupled, extra, port_shift = block_factors(key, index)
        return inverse
    return lax.map(single, jnp.arange(N_BLK * N_SEP)).reshape(N_BLK, N_SEP, NI, NI)


def draw_coupling(key, part):

    def single(index):
        inverse, coupled, extra, port_shift = block_factors(key, index)
        return coupled / jnp.sqrt(NI * 1.0)
    return lax.map(single, jnp.arange(N_BLK * N_SEP)).reshape(N_BLK, N_SEP, NI, PORTS)


def draw_port_matrix(key, part):

    def single(index):
        inverse, coupled, extra, port_shift = block_factors(key, index)
        gamma = 1.25 * largest_value(inverse) + 0.5
        upper = gamma * jnp.dot(coupled.T, coupled, precision=HI) / NI
        return upper + jnp.dot(extra, extra.T, precision=HI) / PORTS + jnp.diag(port_shift)
    return lax.map(single, jnp.arange(N_BLK * N_SEP)).reshape(N_BLK, N_SEP, PORTS, PORTS)


def draw_port_list(key, part):
    half = PORTS // 2
    slots = SEP_PORTS // half

    def single(index):
        base = jax.random.fold_in(jax.random.fold_in(key, 11), index)
        lower = jax.random.permutation(jax.random.fold_in(base, 1), SEP_PORTS)
        higher = jax.random.permutation(jax.random.fold_in(base, 2), SEP_PORTS)
        starts = jnp.arange(N_BLK) % slots * half
        picks = starts[:, None] + jnp.arange(half)[None, :]
        return jnp.concatenate([lower[picks], higher[picks]], axis=1)
    stacked = jax.vmap(single)(jnp.arange(N_SEP))
    return jnp.transpose(stacked, (1, 0, 2)).astype(jnp.int32)


def block_scale(stream_key, shape, cuts, low, high):
    factor_of = 1.0
    for position, blocks in cuts:
        steps = jax.random.uniform(jax.random.fold_in(jax.random.fold_in(stream_key, 6), position), (blocks,), jnp.float32, low / len(cuts), high / len(cuts))
        factor_of = factor_of * jnp.repeat(jnp.exp(steps), shape[position] // blocks).reshape((-1,) + (1,) * (len(shape) - 1 - position))
    return factor_of


def normal_values(key, dims, deviation, reach, cuts=(), kind=jnp.bfloat16):
    factor_of = block_scale(key, dims, cuts, -0.22, 0.18) if cuts else 1.0
    array = jax.random.normal(key, dims, jnp.float32) * deviation * factor_of
    return jnp.minimum(jnp.maximum(array, -reach), reach).astype(kind)


def setup_inputs(seed: int = 0) -> dict:
    key_list = jax.random.split(jax.random.key(seed), 8)
    return {
        "interior_inverse": draw_interior_inverse(jax.random.fold_in(key_list[7], 71), 0),
        "coupling": draw_coupling(jax.random.fold_in(key_list[7], 71), 0),
        "port_matrix": draw_port_matrix(jax.random.fold_in(key_list[7], 71), 0),
        "interior_current": normal_values(key_list[3], (N_BLK, N_SEP, NI, NT), 1.0, 6.0, ((0, 8), (1, 32)), jnp.float32),
        "port_current": normal_values(key_list[4], (N_BLK, N_SEP, PORTS, NT), 1.0, 6.0, ((0, 8), (1, 32)), jnp.float32),
        "port_list": draw_port_list(jax.random.fold_in(key_list[7], 71), 0),
        "spectral_scale": jnp.clip(jax.random.uniform(key_list[6], (), jnp.float32, 1.5, 3.0), 1.5, 3.0),
    }


HI = lax.Precision.HIGHEST


def block_terms(pieces):
    ginv, aip, app, inner, outer = pieces
    width = aip.shape[1]
    solved = jnp.dot(ginv, jnp.concatenate([aip, inner], axis=1), precision=HI)
    reduced = jnp.dot(aip.T, solved, precision=HI)
    return app - reduced[:, :width], outer - reduced[:, width:]


def back_solve(pieces):
    ginv, aip, inner, local = pieces
    return jnp.dot(ginv, inner - jnp.dot(aip, local, precision=HI), precision=HI)


def reference(interior_inverse, coupling, port_matrix, interior_current, port_current, port_list, spectral_scale):
    count = N_BLK * N_SEP
    ginv = interior_inverse.reshape(count, NI, NI)
    aip = coupling.reshape(count, NI, PORTS)
    app = port_matrix.reshape(count, PORTS, PORTS)
    inner = interior_current.reshape(count, NI, NT)
    outer = port_current.reshape(count, PORTS, NT)
    schur, reduced = lax.map(block_terms, (ginv, aip, app, inner, outer))
    sep_index = jnp.arange(N_SEP, dtype=jnp.int32)[None, :, None]
    column = jnp.arange(PORTS, dtype=jnp.int32)[None, None, :]
    owner = jnp.where(column < PORTS // 2, sep_index, (sep_index + 1) % N_SEP)
    global_index = (owner * SEP_PORTS + port_list).astype(jnp.int32).reshape(count, PORTS)
    flat_index = global_index.reshape(-1)
    total = N_SEP * SEP_PORTS

    def matvec(vector):
        local = vector[global_index]
        image = jnp.einsum("bij,bjt->bit", schur, local, precision=HI)
        return jnp.zeros((total, NT), jnp.float32).at[flat_index].add(image.reshape(-1, NT))

    rhs = jnp.zeros((total, NT), jnp.float32).at[flat_index].add(reduced.reshape(-1, NT))
    diagonal_sum = jnp.zeros((total,), jnp.float32).at[flat_index].add(jnp.diagonal(schur, axis1=1, axis2=2).reshape(-1))[:, None]

    def precond(residual):
        level = residual / diagonal_sum
        result = level
        for step in range(DEGREE):
            level = level - matvec(level) / (spectral_scale * diagonal_sum)
            result = result + level
        return result

    solution = jnp.zeros((total, NT), jnp.float32)
    residual = rhs
    search = precond(residual)
    direction = search
    inner_rz = jnp.sum(residual * search, axis=0)
    for step in range(ITERS):
        image = matvec(direction)
        alpha = inner_rz / jnp.sum(direction * image, axis=0)
        solution = solution + alpha * direction
        residual = residual - alpha * image
        if step + 1 < ITERS:
            search = precond(residual)
            newer = jnp.sum(residual * search, axis=0)
            direction = search + (newer / inner_rz) * direction
            inner_rz = newer
    local = solution[global_index]
    interior = lax.map(back_solve, (ginv, aip, inner, local))
    return solution.reshape(N_SEP, SEP_PORTS, NT), interior.reshape(N_BLK, N_SEP, NI, NT)
```

```python
import functools

import jax
import jax.numpy as jnp
from jax import lax
from jax.experimental import pallas as pl
from jax.experimental.pallas import tpu as pltpu
from jax.sharding import PartitionSpec as P

F32 = jnp.float32
BF16 = jnp.bfloat16
HI = lax.Precision.HIGHEST
MID = lax.Precision.HIGH

N_BLK = 8
N_SEP = 32
SETS = 4
HALF = 256
ROWS = 1024
COLS = 16
EXTRA = 8
WHOLE = pl.BlockSpec(memory_space=pltpu.VMEM)
SCALARS = pl.BlockSpec(memory_space=pltpu.SMEM)
ROOM = pltpu.CompilerParams(vmem_limit_bytes=56 * 2**20)


def shifted(array, axis, by, size):
    return lax.ppermute(array, axis, [(i, (i + by) % size) for i in range(size)])


def kernel_call(body, outs, *args, scalars=0):
    shapes = [jax.ShapeDtypeStruct(shape, dtype) for shape, dtype in outs]
    return pl.pallas_call(
        body,
        out_shape=shapes,
        in_specs=[SCALARS] * scalars + [WHOLE] * (len(args) - scalars),
        out_specs=[WHOLE] * len(shapes),
        compiler_params=ROOM,
    )(*args)


def split2(value):
    high = value.astype(BF16)
    return high, (value - high.astype(F32)).astype(BF16)


def dot32(left, right):
    return jnp.dot(left, right, preferred_element_type=F32)


def moved(value, choice):
    rows = value.shape[0]
    high = value.astype(BF16)
    rest = value - high.astype(F32)
    middle = rest.astype(BF16)
    low = (rest - middle.astype(F32)).astype(BF16)
    parts = dot32(jnp.concatenate([high, middle, low], axis=0), choice)
    return parts[:rows] + parts[rows : 2 * rows] + parts[2 * rows :]


def apply_sets(vector, high_ref, low_ref, lower_ref, higher_ref):
    for m in range(SETS):
        at = slice(m * HALF, (m + 1) * HALF)
        piece = jnp.concatenate([vector[:, at], vector[:, ROWS + m * HALF : ROWS + (m + 1) * HALF]], axis=1)
        high, low = split2(piece)
        rows = piece.shape[0]
        both = dot32(jnp.concatenate([high, low], axis=0), high_ref[m])
        image = both[:rows] + both[rows:] + dot32(high, low_ref[m])
        lower_ref[:, at] = image[:, :HALF]
        higher_ref[:, at] = image[:, HALF:]


def matrices_kernel(order_ref, *refs):
    packs, diagonal_ref, high_ref, low_ref = refs[:8], refs[8], refs[9], refs[10]
    row = lax.broadcasted_iota(jnp.int32, (HALF, HALF), 0)
    column = lax.broadcasted_iota(jnp.int32, (HALF, HALF), 1)
    for j in range(SETS):
        m = order_ref[j]
        first = order_ref[SETS + j] == 1
        one, two = packs[j][...], packs[j + SETS][...]
        across = jnp.where(first, one, two)
        packed = jnp.where(first, two, one)
        turned = packed.T
        lower = jnp.where(row <= column, packed, turned)
        higher = jnp.where(row > column, packed, turned)
        higher = jnp.where(row == column, diagonal_ref[m], higher)
        for a, b, part in ((0, 0, lower), (0, 1, across), (1, 0, across.T), (1, 1, higher)):
            at = (m, slice(a * HALF, (a + 1) * HALF), slice(b * HALF, (b + 1) * HALF))
            high, low = split2(part)
            high_ref[at] = high
            low_ref[at] = low


def choice_of(source, target):
    column = jnp.broadcast_to(source, (128, ROWS)).T[:, :1]
    return (column == target).astype(F32).astype(BF16)


def initial_kernel(scale_ref, lower_ref, higher_ref, before_ref, after_ref, into_lower_ref, into_higher_ref, rhs_ref, inverse_ref, damped_ref, level_ref):
    for mine_ref, other_ref, into_ref, side in (
        (lower_ref, before_ref, into_lower_ref, 0),
        (higher_ref, after_ref, into_higher_ref, 1),
    ):
        into_ref[...] = choice_of(other_ref[COLS + 1 : COLS + 2], mine_ref[COLS + 1 : COLS + 2])
        total = mine_ref[...] + moved(other_ref[...], into_ref[...])
        at = slice(side * ROWS, (side + 1) * ROWS)
        inverse = 1.0 / total[COLS : COLS + 1]
        rhs_ref[:, at] = total[:COLS]
        inverse_ref[:, at] = inverse
        damped_ref[:, at] = inverse * (1.0 / scale_ref[0])
        level_ref[:, at] = total[:COLS] * inverse


def assembled(lower_ref, higher_ref, before_ref, after_ref, into_lower_ref, into_higher_ref):
    return jnp.concatenate(
        [
            lower_ref[...] + moved(before_ref[...], into_lower_ref[...]),
            higher_ref[...] + moved(after_ref[...], into_higher_ref[...]),
        ],
        axis=1,
    )


def first_kernel(high_ref, low_ref, level_ref, lower_ref, higher_ref):
    apply_sets(level_ref[...], high_ref, low_ref, lower_ref, higher_ref)


def middle_kernel(high_ref, low_ref, into_lower, into_higher, mine_lower, mine_higher, before, after, damped_ref, level_ref, lower_ref, higher_ref, next_ref, sum_ref):
    image = assembled(mine_lower, mine_higher, before, after, into_lower, into_higher)
    level = level_ref[...] - image * damped_ref[...]
    next_ref[...] = level
    sum_ref[...] = level_ref[...] + level
    apply_sets(level, high_ref, low_ref, lower_ref, higher_ref)


def last_kernel(high_ref, low_ref, into_lower, into_higher, mine_lower, mine_higher, before, after, damped_ref, level_ref, total_ref, lower_ref, higher_ref, result_ref):
    image = assembled(mine_lower, mine_higher, before, after, into_lower, into_higher)
    result = total_ref[...] + (level_ref[...] - image * damped_ref[...])
    result_ref[...] = result
    apply_sets(result, high_ref, low_ref, lower_ref, higher_ref)


def image_kernel(high_ref, low_ref, into_lower, into_higher, mine_lower, mine_higher, before, after, inverse_ref, rhs_ref, search_ref, lower_ref, higher_ref, image_ref, level_ref, sums_ref):
    image = assembled(mine_lower, mine_higher, before, after, into_lower, into_higher)
    image_ref[...] = image
    level = image * inverse_ref[...]
    level_ref[...] = level
    apply_sets(level, high_ref, low_ref, lower_ref, higher_ref)
    search = search_ref[...]
    own = jnp.concatenate([mine_lower[...], mine_higher[...]], axis=1)
    put_sums(
        sums_ref,
        jnp.sum((rhs_ref[...] * search)[:, :ROWS], axis=1, keepdims=True),
        jnp.sum(search * own, axis=1, keepdims=True),
    )


def put_sums(sums_ref, *sums):
    lane = lax.broadcasted_iota(jnp.int32, (COLS, 128), 1)
    out = jnp.zeros((COLS, 128), F32)
    for k, value in enumerate(sums):
        out = jnp.where(lane == k, value, out)
    sums_ref[...] = out


def second_sums_kernel(first_ref, rhs_ref, search_ref, image_ref, turned_ref, q_lower, q_higher, w_lower, w_higher, next_ref, sums_ref):
    alpha = first_ref[:, 0:1] / first_ref[:, 1:2]
    search = search_ref[...]
    following = search - alpha * turned_ref[...]
    next_ref[...] = following
    residual = rhs_ref[:, :ROWS] - alpha * image_ref[:, :ROWS]
    q = jnp.concatenate([q_lower[...], q_higher[...]], axis=1)
    w = q - alpha * jnp.concatenate([w_lower[...], w_higher[...]], axis=1)
    put_sums(
        sums_ref,
        jnp.sum(residual * following[:, :ROWS], axis=1, keepdims=True),
        jnp.sum(following * w, axis=1, keepdims=True),
        jnp.sum(following * q, axis=1, keepdims=True),
        jnp.sum(search * w, axis=1, keepdims=True),
    )


def voltage_kernel(first_ref, second_ref, search_ref, following_ref, names_ref, out_ref):
    rz, pq = first_ref[:, 0:1], first_ref[:, 1:2]
    newer = second_ref[:, 0:1]
    beta = newer / rz
    energy = second_ref[:, 1:2] + beta * (second_ref[:, 2:3] + second_ref[:, 3:4]) + beta * beta * pq
    late = newer / energy
    value = (rz / pq + late * beta) * search_ref[...] + late * following_ref[...]
    natural = lax.broadcasted_iota(jnp.int32, (1, ROWS), 1).astype(F32)
    rows = moved(value[:, :ROWS], choice_of(names_ref[...], natural))
    for b in range(N_BLK):
        m = b % SETS
        out_ref[b, :, :HALF] = value[:, m * HALF : (m + 1) * HALF]
        out_ref[b, :, HALF : 2 * HALF] = value[:, ROWS + m * HALF : ROWS + (m + 1) * HALF]
        out_ref[b, :, 2 * HALF :] = rows[:, b * 128 : (b + 1) * 128]


def group_sum(values):
    for d in (1, 2, 4, 8, 16):
        values = values + lax.ppermute(values, "sep", [(i, i ^ d) for i in range(N_SEP)])
    return values


def body(interior_inverse, coupling, port_matrix, interior_current, port_current, port_list, spectral_scale):
    ginv = interior_inverse[0, 0]
    aip = coupling[0, 0]
    app = port_matrix[0, 0]
    inner = interior_current[0, 0]
    outer = port_current[0, 0]
    ports = port_list[0, 0]
    b = lax.axis_index("blk")

    halves = (ports[:HALF], ports[HALF:])
    places = jnp.arange(HALF, dtype=jnp.int32)
    orders = []
    for half in halves:
        rank = jnp.sum((half[None, :] < half[:, None]).astype(jnp.int32), axis=1)
        orders.append((rank[:, None] == places[None, :]).astype(F32))
    names = jnp.concatenate(
        [jnp.sum(order * half.astype(F32)[:, None], axis=0) for order, half in zip(orders, halves)]
    )

    def sorted_columns(array):
        return jnp.concatenate(
            [jnp.dot(array[:, :HALF], orders[0], precision=HI), jnp.dot(array[:, HALF:], orders[1], precision=HI)],
            axis=1,
        )

    aip = sorted_columns(aip)
    app = sorted_columns(sorted_columns(app).T)
    solved = jnp.dot(ginv, aip, precision=MID)
    schur = app - jnp.dot(aip.T, solved, precision=MID)
    reduced = sorted_columns(outer.T) - jnp.dot(inner.T, solved, precision=MID)
    own_inner = jnp.dot(ginv, inner, precision=MID)

    across = schur[:HALF, HALF:]
    packed = jnp.where(places[:, None] <= places[None, :], schur[:HALF, :HALF], schur[HALF:, HALF:])
    eye = places[:, None] == places[None, :]
    diagonal = jnp.concatenate(
        [jnp.sum(jnp.where(eye, schur[:HALF, :HALF], 0.0), axis=0), jnp.sum(jnp.where(eye, schur[HALF:, HALF:], 0.0), axis=0)]
    )
    early = b < SETS
    got = shifted(jnp.where(early, packed, across), "blk", SETS, N_BLK)
    mine = jnp.where(early, across, packed) + got
    packs = [mine] + [shifted(mine, "blk", d, N_BLK) for d in range(1, N_BLK)]

    extra = jnp.concatenate([diagonal[None], names[None], jnp.zeros((EXTRA - 2, 2 * HALF), F32)], axis=0)
    message = jnp.concatenate(
        [reduced.reshape(N_BLK, COLS, 2 * HALF), jnp.broadcast_to(extra[None], (N_BLK, EXTRA, 2 * HALF))], axis=1
    )
    parts = lax.all_to_all(message, "blk", 0, 0, tiled=True)
    sums = parts[:SETS] + parts[SETS:]
    by_rows = jnp.transpose(sums, (1, 0, 2))
    lower = by_rows[:, :, :HALF].reshape(COLS + EXTRA, ROWS)
    higher = by_rows[:, :, HALF:].reshape(COLS + EXTRA, ROWS)
    before = shifted(higher, "sep", 1, N_SEP)
    after = shifted(lower, "sep", -1, N_SEP)
    vec = ((COLS, 2 * ROWS), F32)
    line = ((1, 2 * ROWS), F32)
    side = ((COLS, ROWS), F32)
    choice = ((ROWS, ROWS), BF16)
    into_lower, into_higher, rhs, inverse, damped, level = kernel_call(
        initial_kernel, [choice, choice, vec, line, line, vec], spectral_scale.reshape(1), lower, higher, before, after, scalars=1
    )
    at = jnp.arange(SETS, dtype=jnp.int32)
    order = jnp.concatenate([(b - at) % SETS, ((b - at) % N_BLK < SETS).astype(jnp.int32)])
    matrices = kernel_call(
        matrices_kernel,
        [((SETS, 2 * HALF, 2 * HALF), BF16)] * 2,
        order,
        *packs,
        sums[:, COLS : COLS + 1, HALF:],
        scalars=1,
    )

    def exchanged(low, high):
        return low, high, shifted(high, "sep", 1, N_SEP), shifted(low, "sep", -1, N_SEP)

    def preconditioned(level, low, high):
        low, high, level, total = kernel_call(
            middle_kernel, [side, side, vec, vec], *matrices, into_lower, into_higher, *exchanged(low, high), damped, level
        )
        return kernel_call(
            last_kernel, [side, side, vec], *matrices, into_lower, into_higher, *exchanged(low, high), damped, level, total
        )

    low, high = kernel_call(first_kernel, [side, side], *matrices, level)
    q_low, q_high, search = preconditioned(level, low, high)
    low, high, image, level, first = kernel_call(
        image_kernel,
        [side, side, vec, vec, ((COLS, 128), F32)],
        *matrices, into_lower, into_higher, *exchanged(q_low, q_high), inverse, rhs, search,
    )
    first = group_sum(first)
    w_low, w_high, turned = preconditioned(level, low, high)
    following, second = kernel_call(
        second_sums_kernel, [vec, ((COLS, 128), F32)], first, rhs, search, image, turned, q_low, q_high, w_low, w_high
    )
    second = group_sum(second)
    own_names = 0.5 * lower[COLS + 1 : COLS + 2]
    (spread,) = kernel_call(
        voltage_kernel, [((N_BLK, COLS, 640), F32)], first, second, search, following, own_names
    )
    voltage = lax.all_to_all(spread, "blk", 0, 0, tiled=True).reshape(128, 640)
    local = voltage[:, : 2 * HALF]
    interior = own_inner - lax.dot_general(solved, local, (((1,), (1,)), ((), ())), precision=MID)
    return voltage[:, 2 * HALF :].T[None], interior[None, None]


def solution(mesh):
    return jax.shard_map(
        body,
        mesh=mesh,
        in_specs=(
            P("blk", "sep", None, None),
            P("blk", "sep", None, None),
            P("blk", "sep", None, None),
            P("blk", "sep", None, None),
            P("blk", "sep", None, None),
            P("blk", "sep", None),
            P(),
        ),
        out_specs=(P("sep", "blk", None), P("blk", "sep", None, None)),
        check_vma=False,
    )
```

```python
import functools

import jax
import jax.numpy as jnp
from jax import lax
from jax.experimental import pallas as pl
from jax.experimental.pallas import tpu as pltpu
from jax.sharding import PartitionSpec as P

F32 = jnp.float32
BF16 = jnp.bfloat16
HI = lax.Precision.HIGHEST
MID = lax.Precision.HIGH

N_BLK = 8
N_SEP = 32
SETS = 4
HALF = 256
ROWS = 1024
NI = 1024
COLS = 16
EXTRA = 8
WHOLE = pl.BlockSpec(memory_space=pltpu.VMEM)
SCALARS = pl.BlockSpec(memory_space=pltpu.SMEM)
ROOM = pltpu.CompilerParams(vmem_limit_bytes=56 * 2**20)


def shifted(array, axis, by, size):
    return lax.ppermute(array, axis, [(i, (i + by) % size) for i in range(size)])


def kernel_call(body, outs, *args, scalars=0):
    shapes = [jax.ShapeDtypeStruct(shape, dtype) for shape, dtype in outs]
    return pl.pallas_call(
        body,
        out_shape=shapes,
        in_specs=[SCALARS] * scalars + [WHOLE] * (len(args) - scalars),
        out_specs=[WHOLE] * len(shapes),
        compiler_params=ROOM,
    )(*args)


def split2(value):
    high = value.astype(BF16)
    return high, (value - high.astype(F32)).astype(BF16)


def dot32(left, right):
    return jnp.dot(left, right, preferred_element_type=F32)


def moved(value, choice):
    rows = value.shape[0]
    high = value.astype(BF16)
    rest = value - high.astype(F32)
    middle = rest.astype(BF16)
    low = (rest - middle.astype(F32)).astype(BF16)
    parts = dot32(jnp.concatenate([high, middle, low], axis=0), choice)
    return parts[:rows] + parts[rows : 2 * rows] + parts[2 * rows :]


def places_of(source, target):
    column = jnp.broadcast_to(source, (128, ROWS)).T[:, :1]
    at = lax.broadcasted_iota(jnp.int32, (ROWS, 1), 0).astype(F32)
    return jnp.sum(jnp.where(column == target, at, 0.0), axis=0, keepdims=True).astype(jnp.int32)


def taken(value, places):
    rows = value.shape[0]
    out = []
    for j in range(ROWS // 128):
        place = jnp.broadcast_to(places[:, j * 128 : (j + 1) * 128], (rows, 128))
        lane, tile = place & 127, place >> 7
        result = jnp.zeros((rows, 128), F32)
        for k in range(ROWS // 128):
            piece = jnp.take_along_axis(value[:, k * 128 : (k + 1) * 128], lane, axis=1)
            result = jnp.where(tile == k, piece, result)
        out.append(result)
    return jnp.concatenate(out, axis=1)


def apply_sets(vector, high_ref, low_ref, lower_ref, higher_ref):
    for m in range(SETS):
        at = slice(m * HALF, (m + 1) * HALF)
        piece = jnp.concatenate([vector[:, at], vector[:, ROWS + m * HALF : ROWS + (m + 1) * HALF]], axis=1)
        high, low = split2(piece)
        rows = piece.shape[0]
        both = dot32(jnp.concatenate([high, low], axis=0), high_ref[m])
        image = both[:rows] + both[rows:] + dot32(high, low_ref[m])
        lower_ref[:, at] = image[:, :HALF]
        higher_ref[:, at] = image[:, HALF:]


def matrices_kernel(order_ref, *refs):
    packs, diagonal_ref, high_ref, low_ref = refs[:8], refs[8], refs[9], refs[10]
    row = lax.broadcasted_iota(jnp.int32, (HALF, HALF), 0)
    column = lax.broadcasted_iota(jnp.int32, (HALF, HALF), 1)
    for j in range(SETS):
        m = order_ref[j]
        first = order_ref[SETS + j] == 1
        one, two = packs[2 * j][...], packs[2 * j + 1][...]
        across = jnp.where(first, one, two)
        packed = jnp.where(first, two, one)
        turned = packed.T
        lower = jnp.where(row <= column, packed, turned)
        higher = jnp.where(row > column, packed, turned)
        higher = jnp.where(row == column, diagonal_ref[m], higher)
        for a, b, part in ((0, 0, lower), (0, 1, across), (1, 0, across.T), (1, 1, higher)):
            at = (m, slice(a * HALF, (a + 1) * HALF), slice(b * HALF, (b + 1) * HALF))
            high, low = split2(part)
            high_ref[at] = high
            low_ref[at] = low


def initial_kernel(scale_ref, lower_ref, higher_ref, before_ref, after_ref, into_lower_ref, into_higher_ref, rhs_ref, inverse_ref, damped_ref, level_ref):
    for mine_ref, other_ref, into_ref, side in (
        (lower_ref, before_ref, into_lower_ref, 0),
        (higher_ref, after_ref, into_higher_ref, 1),
    ):
        places = places_of(other_ref[COLS + 1 : COLS + 2], mine_ref[COLS + 1 : COLS + 2])
        into_ref[...] = places
        total = mine_ref[...] + taken(other_ref[...], places)
        at = slice(side * ROWS, (side + 1) * ROWS)
        inverse = 1.0 / total[COLS : COLS + 1]
        rhs_ref[:, at] = total[:COLS]
        inverse_ref[:, at] = inverse
        damped_ref[:, at] = inverse * (1.0 / scale_ref[0])
        level_ref[:, at] = total[:COLS] * inverse


def assembled(lower_ref, higher_ref, before_ref, after_ref, into_lower_ref, into_higher_ref):
    return jnp.concatenate(
        [
            lower_ref[...] + taken(before_ref[...], into_lower_ref[...]),
            higher_ref[...] + taken(after_ref[...], into_higher_ref[...]),
        ],
        axis=1,
    )


def first_kernel(high_ref, low_ref, level_ref, lower_ref, higher_ref):
    apply_sets(level_ref[...], high_ref, low_ref, lower_ref, higher_ref)


def middle_kernel(high_ref, low_ref, into_lower, into_higher, mine_lower, mine_higher, before, after, damped_ref, level_ref, lower_ref, higher_ref, next_ref, sum_ref):
    image = assembled(mine_lower, mine_higher, before, after, into_lower, into_higher)
    level = level_ref[...] - image * damped_ref[...]
    next_ref[...] = level
    sum_ref[...] = level_ref[...] + level
    apply_sets(level, high_ref, low_ref, lower_ref, higher_ref)


def last_kernel(high_ref, low_ref, into_lower, into_higher, mine_lower, mine_higher, before, after, damped_ref, level_ref, total_ref, lower_ref, higher_ref, result_ref):
    image = assembled(mine_lower, mine_higher, before, after, into_lower, into_higher)
    result = total_ref[...] + (level_ref[...] - image * damped_ref[...])
    result_ref[...] = result
    apply_sets(result, high_ref, low_ref, lower_ref, higher_ref)


def image_kernel(high_ref, low_ref, into_lower, into_higher, mine_lower, mine_higher, before, after, inverse_ref, lower_ref, higher_ref, image_ref, level_ref):
    image = assembled(mine_lower, mine_higher, before, after, into_lower, into_higher)
    image_ref[...] = image
    level = image * inverse_ref[...]
    level_ref[...] = level
    apply_sets(level, high_ref, low_ref, lower_ref, higher_ref)


def two_sum(a, b):
    total = a + b
    part = total - a
    return total, (a - (total - part)) + (b - part)


def halves_of(a):
    scaled = a * 4097.0
    high = scaled - (scaled - a)
    return high, a - high


def two_product(a, b):
    product = a * b
    a_high, a_low = halves_of(a)
    b_high, b_low = halves_of(b)
    return product, ((a_high * b_high - product) + a_high * b_low + a_low * b_high) + a_low * b_low


def double_add(a, b):
    total, rest = two_sum(a[0], b[0])
    return two_sum(total, rest + (a[1] + b[1]))


def double_scaled(a, factor):
    total, rest = two_product(a[0], factor)
    return two_sum(total, rest + a[1] * factor)


def inner_product(left, right):
    total = jnp.zeros((COLS, 128), F32)
    rest = jnp.zeros((COLS, 128), F32)
    for k in range(left.shape[1] // 128):
        at = slice(k * 128, (k + 1) * 128)
        product, lost = two_product(left[:, at], right[:, at])
        total, also = two_sum(total, product)
        rest = rest + (lost + also)
    return total, rest


def inner_products(pairs, out_ref):
    results = [inner_product(left, right) for left, right in pairs]
    total = jnp.concatenate([result[0] for result in results], axis=0).T
    rest = jnp.concatenate([result[1] for result in results], axis=0).T
    rows = 64
    while rows >= 8:
        total, lost = two_sum(total[:rows], total[rows:])
        rest = (rest[:rows] + rest[rows:]) + lost
        rows //= 2
    for by in (4, 2, 1):
        total, lost = two_sum(total, pltpu.roll(total, by, 0))
        rest = (rest + pltpu.roll(rest, by, 0)) + lost
    row = lax.broadcasted_iota(jnp.int32, (8, 128), 0)
    message = jnp.where(row == 0, total, jnp.where(row == 1, rest, 0.0))
    for k in range(N_SEP):
        out_ref[k] = message


def closing_kernel(high_ref, low_ref, into_lower, into_higher, mine_lower, mine_higher, before, after, damped_ref, level_ref, total_ref, rhs_ref, search_ref, image_ref, q_lower, q_higher, result_ref, out_ref, w_lower, w_higher):
    image = assembled(mine_lower, mine_higher, before, after, into_lower, into_higher)
    result = total_ref[...] + (level_ref[...] - image * damped_ref[...])
    result_ref[...] = result
    apply_sets(result, high_ref, low_ref, w_lower, w_higher)
    q = jnp.concatenate([q_lower[...], q_higher[...]], axis=1)
    w = jnp.concatenate([w_lower[...], w_higher[...]], axis=1)
    search = search_ref[...]
    rhs, image = rhs_ref[:, :ROWS], image_ref[:, :ROWS]
    own_search, own_result = search[:, :ROWS], result[:, :ROWS]
    inner_products(
        [
            (rhs, own_search),
            (rhs, own_result),
            (image, own_search),
            (image, own_result),
            (search, q),
            (search, w),
            (result, q),
            (result, w),
        ],
        out_ref,
    )


def voltage_kernel(sums_ref, search_ref, turned_ref, names_ref, out_ref):
    total = sums_ref[0]
    rest = jnp.zeros((8, 128), F32)
    for k in range(1, N_SEP):
        total, lost = two_sum(total, sums_ref[k])
        rest = rest + lost
    rest = rest[0:1] + total[1:2]
    columns = [jnp.broadcast_to(line, (128, 128)).T[:, :1] for line in (total[0:1], rest)]
    rz, ru, qz, qu, zq, zw, uq, uw = [
        two_sum(*(column[k * COLS : (k + 1) * COLS] for column in columns)) for k in range(8)
    ]
    alpha = rz[0] / zq[0]
    newer = double_add(
        double_add(rz, double_scaled(double_add(ru, qz), -alpha)), double_scaled(double_scaled(qu, alpha), alpha)
    )[0]
    late_late = double_add(
        double_add(zq, double_scaled(double_add(zw, uq), -alpha)), double_scaled(double_scaled(uw, alpha), alpha)
    )[0]
    late_early = double_add(zq, double_scaled(uq, -alpha))[0]
    early_late = double_add(zq, double_scaled(zw, -alpha))[0]
    beta = newer / rz[0]
    energy = late_late + beta * (late_early + early_late) + beta * beta * zq[0]
    late = newer / energy
    search = search_ref[...]
    value = (alpha + late * beta) * search + late * (search - alpha * turned_ref[...])
    natural = lax.broadcasted_iota(jnp.int32, (1, ROWS), 1).astype(F32)
    rows = taken(value[:, :ROWS], places_of(names_ref[...], natural))
    for b in range(N_BLK):
        m = b % SETS
        out_ref[b, :, :HALF] = value[:, m * HALF : (m + 1) * HALF]
        out_ref[b, :, HALF : 2 * HALF] = value[:, ROWS + m * HALF : ROWS + (m + 1) * HALF]
        out_ref[b, :, 2 * HALF :] = rows[:, b * 128 : (b + 1) * 128]


def sort_kernel(early_ref, ports_ref, schur_ref, outer_ref, product_ref, keep_ref, send_ref, message_ref, low_order_ref, high_order_ref):
    row = lax.broadcasted_iota(jnp.int32, (HALF, HALF), 0)
    column = lax.broadcasted_iota(jnp.int32, (HALF, HALF), 1)
    reduced = outer_ref[...].T - product_ref[...]
    into, moved_sides = [], []
    for side, order_ref in ((0, low_order_ref), (1, high_order_ref)):
        at = slice(side * HALF, (side + 1) * HALF)
        names = ports_ref[:, at].astype(F32)
        across = jnp.broadcast_to(names, (HALF, HALF))
        rank = jnp.sum((across.T < across).astype(F32), axis=0, keepdims=True)
        order = (row.astype(F32) == rank).astype(F32)
        order_ref[...] = order.astype(BF16)
        into.append(order.T.astype(BF16))
        moved_sides.append(moved(jnp.concatenate([reduced[:, at], jnp.broadcast_to(names, (8, HALF))], axis=0), into[side]))
    lower = moved(moved(schur_ref[:HALF, :HALF], into[0]).T, into[0])
    higher = moved(moved(schur_ref[HALF:, HALF:], into[1]).T, into[1])
    across = moved(moved(schur_ref[HALF:, :HALF], into[0]).T, into[1])
    packed = jnp.where(row <= column, lower, higher)
    early = early_ref[0] == 1
    keep_ref[...] = jnp.where(early, across, packed)
    send_ref[...] = jnp.where(early, packed, across)
    extra_row = lax.broadcasted_iota(jnp.int32, (EXTRA, HALF), 0)
    for side, matrix in ((0, lower), (1, higher)):
        at = slice(side * HALF, (side + 1) * HALF)
        diagonal = jnp.sum(jnp.where(row == column, matrix, 0.0), axis=0, keepdims=True)
        names = moved_sides[side][128:]
        extra = jnp.where(extra_row == 0, diagonal, jnp.where(extra_row == 1, names, 0.0))
        for c in range(N_BLK):
            message_ref[c, :COLS, at] = moved_sides[side][c * COLS : (c + 1) * COLS]
            message_ref[c, COLS:, at] = extra


def split_kernel(value_ref, high_ref, low_ref):
    high_ref[...], low_ref[...] = split2(value_ref[...])


def interior_kernel(voltage_ref, low_order_ref, high_order_ref, high_ref, low_ref, inner_ref, interior_ref, port_ref):
    local = jnp.concatenate(
        [moved(voltage_ref[:, :HALF], low_order_ref[...]), moved(voltage_ref[:, HALF : 2 * HALF], high_order_ref[...])],
        axis=1,
    )
    high, low = split2(local)

    def turned(left, right):
        return lax.dot_general(left, right, (((1,), (1,)), ((), ())), preferred_element_type=F32)

    solved = high_ref[...]
    interior_ref[...] = inner_ref[...] - (turned(solved, high) + (turned(solved, low) + turned(low_ref[...], high)))
    port_ref[...] = voltage_ref[:, 2 * HALF :].T


def body(interior_inverse, coupling, port_matrix, interior_current, port_current, port_list, spectral_scale):
    ginv = interior_inverse[0, 0]
    aip = coupling[0, 0]
    app = port_matrix[0, 0]
    inner = interior_current[0, 0]
    outer = port_current[0, 0]
    ports = port_list[0, 0]
    b = lax.axis_index("blk")

    solved = jnp.dot(ginv, aip, precision=MID)
    schur = app - jnp.dot(aip.T, solved, precision=MID)
    product = jnp.dot(inner.T, solved, precision=MID)
    own_inner = jnp.dot(ginv, inner, precision=MID)

    square = ((HALF, HALF), F32)
    order = ((HALF, HALF), BF16)
    keep, send, message, low_order, high_order = kernel_call(
        sort_kernel,
        [square, square, ((N_BLK, COLS + EXTRA, 2 * HALF), F32), order, order],
        (b < SETS).astype(jnp.int32).reshape(1),
        ports.reshape(1, 2 * HALF),
        schur,
        outer,
        product,
        scalars=1,
    )
    mine = keep + shifted(send, "blk", SETS, N_BLK)
    packs = [mine] + [shifted(mine, "blk", d, N_BLK) for d in (4, 2, 6)]
    packs = packs + [lax.ppermute(pack, "blk", [(i, i ^ 1) for i in range(N_BLK)]) for pack in packs]
    sources = [b, (b - 2) % N_BLK, b ^ 1, ((b ^ 1) - 2) % N_BLK]

    parts = lax.all_to_all(message, "blk", 0, 0, tiled=True)
    sums = parts[:SETS] + parts[SETS:]
    by_rows = jnp.transpose(sums, (1, 0, 2))
    lower = by_rows[:, :, :HALF].reshape(COLS + EXTRA, ROWS)
    higher = by_rows[:, :, HALF:].reshape(COLS + EXTRA, ROWS)
    before = shifted(higher, "sep", 1, N_SEP)
    after = shifted(lower, "sep", -1, N_SEP)
    solved_high, solved_low = kernel_call(split_kernel, [((NI, 2 * HALF), BF16)] * 2, solved)
    before, after, own_inner, solved_high, solved_low = lax.optimization_barrier(
        (before, after, own_inner, solved_high, solved_low)
    )
    vec = ((COLS, 2 * ROWS), F32)
    line = ((1, 2 * ROWS), F32)
    side = ((COLS, ROWS), F32)
    choice = ((1, ROWS), jnp.int32)
    into_lower, into_higher, rhs, inverse, damped, level = kernel_call(
        initial_kernel, [choice, choice, vec, line, line, vec], spectral_scale.reshape(1), lower, higher, before, after, scalars=1
    )
    order = jnp.stack([source % SETS for source in sources] + [(source < SETS).astype(jnp.int32) for source in sources])
    matrices = kernel_call(
        matrices_kernel,
        [((SETS, 2 * HALF, 2 * HALF), BF16)] * 2,
        order,
        *packs,
        sums[:, COLS : COLS + 1, HALF:],
        scalars=1,
    )

    def exchanged(low, high):
        return low, high, shifted(high, "sep", 1, N_SEP), shifted(low, "sep", -1, N_SEP)

    def applied(kernel, outs, low, high, *others):
        return kernel_call(kernel, outs, *matrices, into_lower, into_higher, *exchanged(low, high), *others)

    low, high = kernel_call(first_kernel, [side, side], *matrices, level)
    low, high, level, total = applied(middle_kernel, [side, side, vec, vec], low, high, damped, level)
    q_low, q_high, search = applied(last_kernel, [side, side, vec], low, high, damped, level, total)
    low, high, image, level = applied(image_kernel, [side, side, vec, vec], q_low, q_high, inverse)
    low, high, level, total = applied(middle_kernel, [side, side, vec, vec], low, high, damped, level)
    turned, products, _, _ = applied(
        closing_kernel,
        [vec, ((N_SEP, 8, 128), F32), side, side],
        low, high, damped, level, total, rhs, search, image, q_low, q_high,
    )
    products = lax.all_to_all(products, "sep", 0, 0, tiled=True)
    own_names = 0.5 * lower[COLS + 1 : COLS + 2]
    (spread,) = kernel_call(voltage_kernel, [((N_BLK, COLS, 640), F32)], products, search, turned, own_names)
    voltage = lax.all_to_all(spread, "blk", 0, 0, tiled=True).reshape(128, 640)
    interior, port = kernel_call(
        interior_kernel, [((NI, 128), F32), ((128, 128), F32)], voltage, low_order, high_order, solved_high, solved_low, own_inner
    )
    return port[None], interior[None, None]


def solution(mesh):
    return jax.shard_map(
        body,
        mesh=mesh,
        in_specs=(
            P("blk", "sep", None, None),
            P("blk", "sep", None, None),
            P("blk", "sep", None, None),
            P("blk", "sep", None, None),
            P("blk", "sep", None, None),
            P("blk", "sep", None),
            P(),
        ),
        out_specs=(P("sep", "blk", None), P("blk", "sep", None, None)),
        check_vma=False,
    )
```

```python
import functools

import jax
import jax.numpy as jnp
from jax import lax
from jax.experimental import pallas as pl
from jax.experimental.pallas import tpu as pltpu
from jax.sharding import PartitionSpec as P

F32 = jnp.float32
BF16 = jnp.bfloat16
HI = lax.Precision.HIGHEST
MID = lax.Precision.HIGH

N_BLK = 8
N_SEP = 32
SETS = 4
HALF = 256
ROWS = 1024
NI = 1024
COLS = 16
EXTRA = 8
WHOLE = pl.BlockSpec(memory_space=pltpu.VMEM)
SCALARS = pl.BlockSpec(memory_space=pltpu.SMEM)
ROOM = pltpu.CompilerParams(vmem_limit_bytes=20 * 2**20)


def shifted(array, axis, by, size):
    return lax.ppermute(array, axis, [(i, (i + by) % size) for i in range(size)])


def kernel_call(body, outs, *args, scalars=0):
    shapes = [jax.ShapeDtypeStruct(shape, dtype) for shape, dtype in outs]
    return pl.pallas_call(
        body,
        out_shape=shapes,
        in_specs=[SCALARS] * scalars + [WHOLE] * (len(args) - scalars),
        out_specs=[WHOLE] * len(shapes),
        compiler_params=ROOM,
    )(*args)


def split2(value):
    high = value.astype(BF16)
    return high, (value - high.astype(F32)).astype(BF16)


def dot32(left, right):
    return jnp.dot(left, right, preferred_element_type=F32)


def moved(value, choice):
    rows = value.shape[0]
    high = value.astype(BF16)
    rest = value - high.astype(F32)
    middle = rest.astype(BF16)
    low = (rest - middle.astype(F32)).astype(BF16)
    parts = dot32(jnp.concatenate([high, middle, low], axis=0), choice)
    return parts[:rows] + parts[rows : 2 * rows] + parts[2 * rows :]


def places_of(source, target):
    column = jnp.broadcast_to(source, (128, ROWS)).T[:, :1]
    at = lax.broadcasted_iota(jnp.int32, (ROWS, 1), 0).astype(F32)
    return jnp.sum(jnp.where(column == target, at, 0.0), axis=0, keepdims=True).astype(jnp.int32)


def taken(value, places):
    rows = value.shape[0]
    out = []
    for j in range(ROWS // 128):
        place = jnp.broadcast_to(places[:, j * 128 : (j + 1) * 128], (rows, 128))
        lane, tile = place & 127, place >> 7
        result = jnp.zeros((rows, 128), F32)
        for k in range(ROWS // 128):
            piece = jnp.take_along_axis(value[:, k * 128 : (k + 1) * 128], lane, axis=1)
            result = jnp.where(tile == k, piece, result)
        out.append(result)
    return jnp.concatenate(out, axis=1)


def apply_set(piece, high_matrix, low_matrix):
    high, low = split2(piece)
    rows = piece.shape[0]
    both = dot32(jnp.concatenate([high, low], axis=0), high_matrix)
    return both[:rows] + both[rows:] + dot32(high, low_matrix)


def apply_sets(vector, high_ref, low_ref, lower_ref, higher_ref):
    for m in range(SETS):
        at = slice(m * HALF, (m + 1) * HALF)
        piece = jnp.concatenate([vector[:, at], vector[:, ROWS + m * HALF : ROWS + (m + 1) * HALF]], axis=1)
        image = apply_set(piece, high_ref[m], low_ref[m])
        lower_ref[:, at] = image[:, :HALF]
        higher_ref[:, at] = image[:, HALF:]


def matrices_kernel(order_ref, *refs):
    packs, (diagonal_ref, level_ref, high_ref, low_ref, lower_ref, higher_ref) = refs[:8], refs[8:]
    row = lax.broadcasted_iota(jnp.int32, (HALF, HALF), 0)
    column = lax.broadcasted_iota(jnp.int32, (HALF, HALF), 1)
    for j in range(SETS):
        m = order_ref[j]
        first = order_ref[SETS + j] == 1
        one, two = packs[2 * j][...], packs[2 * j + 1][...]
        across = jnp.where(first, one, two)
        packed = jnp.where(first, two, one)
        turned = packed.T
        lower = jnp.where(row <= column, packed, turned)
        higher = jnp.where(row > column, packed, turned)
        higher = jnp.where(row == column, diagonal_ref[m], higher)
        for a, b, part in ((0, 0, lower), (0, 1, across), (1, 0, across.T), (1, 1, higher)):
            at = (m, slice(a * HALF, (a + 1) * HALF), slice(b * HALF, (b + 1) * HALF))
            high, low = split2(part)
            high_ref[at] = high
            low_ref[at] = low
        start = pl.multiple_of(m * HALF, HALF)
        image = apply_set(
            jnp.concatenate([level_ref[:, pl.ds(start, HALF)], level_ref[:, pl.ds(ROWS + start, HALF)]], axis=1),
            high_ref[m],
            low_ref[m],
        )
        lower_ref[:, pl.ds(start, HALF)] = image[:, :HALF]
        higher_ref[:, pl.ds(start, HALF)] = image[:, HALF:]


def initial_kernel(scale_ref, lower_ref, higher_ref, before_ref, after_ref, into_lower_ref, into_higher_ref, rhs_ref, inverse_ref, damped_ref, level_ref):
    for mine_ref, other_ref, into_ref, side in (
        (lower_ref, before_ref, into_lower_ref, 0),
        (higher_ref, after_ref, into_higher_ref, 1),
    ):
        places = places_of(other_ref[COLS + 1 : COLS + 2], mine_ref[COLS + 1 : COLS + 2])
        into_ref[...] = places
        total = mine_ref[...] + taken(other_ref[...], places)
        at = slice(side * ROWS, (side + 1) * ROWS)
        inverse = 1.0 / total[COLS : COLS + 1]
        rhs_ref[:, at] = total[:COLS]
        inverse_ref[:, at] = inverse
        damped_ref[:, at] = inverse * (1.0 / scale_ref[0])
        level_ref[:, at] = total[:COLS] * inverse


def assembled(lower_ref, higher_ref, before_ref, after_ref, into_lower_ref, into_higher_ref):
    return jnp.concatenate(
        [
            lower_ref[...] + taken(before_ref[...], into_lower_ref[...]),
            higher_ref[...] + taken(after_ref[...], into_higher_ref[...]),
        ],
        axis=1,
    )


def middle_kernel(high_ref, low_ref, into_lower, into_higher, mine_lower, mine_higher, before, after, damped_ref, level_ref, lower_ref, higher_ref, next_ref, sum_ref):
    image = assembled(mine_lower, mine_higher, before, after, into_lower, into_higher)
    level = level_ref[...] - image * damped_ref[...]
    next_ref[...] = level
    sum_ref[...] = level_ref[...] + level
    apply_sets(level, high_ref, low_ref, lower_ref, higher_ref)


def last_kernel(high_ref, low_ref, into_lower, into_higher, mine_lower, mine_higher, before, after, damped_ref, level_ref, total_ref, lower_ref, higher_ref, result_ref):
    image = assembled(mine_lower, mine_higher, before, after, into_lower, into_higher)
    result = total_ref[...] + (level_ref[...] - image * damped_ref[...])
    result_ref[...] = result
    apply_sets(result, high_ref, low_ref, lower_ref, higher_ref)


def image_kernel(high_ref, low_ref, into_lower, into_higher, mine_lower, mine_higher, before, after, inverse_ref, lower_ref, higher_ref, image_ref, level_ref):
    image = assembled(mine_lower, mine_higher, before, after, into_lower, into_higher)
    image_ref[...] = image
    level = image * inverse_ref[...]
    level_ref[...] = level
    apply_sets(level, high_ref, low_ref, lower_ref, higher_ref)


def two_sum(a, b):
    total = a + b
    part = total - a
    return total, (a - (total - part)) + (b - part)


def halves_of(a):
    scaled = a * 4097.0
    high = scaled - (scaled - a)
    return high, a - high


def two_product(a, b):
    product = a * b
    a_high, a_low = halves_of(a)
    b_high, b_low = halves_of(b)
    return product, ((a_high * b_high - product) + a_high * b_low + a_low * b_high) + a_low * b_low


def double_add(a, b):
    total, rest = two_sum(a[0], b[0])
    return two_sum(total, rest + (a[1] + b[1]))


def double_scaled(a, factor):
    total, rest = two_product(a[0], factor)
    return two_sum(total, rest + a[1] * factor)


def inner_product(left, right):
    total = jnp.zeros((COLS, 128), F32)
    rest = jnp.zeros((COLS, 128), F32)
    for k in range(left.shape[1] // 128):
        at = slice(k * 128, (k + 1) * 128)
        product, lost = two_product(left[:, at], right[:, at])
        total, also = two_sum(total, product)
        rest = rest + (lost + also)
    return total, rest


def inner_products(pairs, out_ref):
    results = [inner_product(left, right) for left, right in pairs]
    total = jnp.concatenate([result[0] for result in results], axis=0).T
    rest = jnp.concatenate([result[1] for result in results], axis=0).T
    rows = 64
    while rows >= 8:
        total, lost = two_sum(total[:rows], total[rows:])
        rest = (rest[:rows] + rest[rows:]) + lost
        rows //= 2
    for by in (4, 2, 1):
        total, lost = two_sum(total, pltpu.roll(total, by, 0))
        rest = (rest + pltpu.roll(rest, by, 0)) + lost
    row = lax.broadcasted_iota(jnp.int32, (8, 128), 0)
    message = jnp.where(row == 0, total, jnp.where(row == 1, rest, 0.0))
    for k in range(N_SEP):
        out_ref[k] = message


def closing_kernel(high_ref, low_ref, into_lower, into_higher, mine_lower, mine_higher, before, after, damped_ref, level_ref, total_ref, rhs_ref, search_ref, image_ref, q_lower, q_higher, result_ref, out_ref, w_lower, w_higher):
    image = assembled(mine_lower, mine_higher, before, after, into_lower, into_higher)
    result = total_ref[...] + (level_ref[...] - image * damped_ref[...])
    result_ref[...] = result
    apply_sets(result, high_ref, low_ref, w_lower, w_higher)
    q = jnp.concatenate([q_lower[...], q_higher[...]], axis=1)
    w = jnp.concatenate([w_lower[...], w_higher[...]], axis=1)
    search = search_ref[...]
    rhs, image = rhs_ref[:, :ROWS], image_ref[:, :ROWS]
    own_search, own_result = search[:, :ROWS], result[:, :ROWS]
    inner_products(
        [
            (rhs, own_search),
            (rhs, own_result),
            (image, own_search),
            (image, own_result),
            (search, q),
            (search, w),
            (result, q),
            (result, w),
        ],
        out_ref,
    )


def voltage_kernel(sums_ref, search_ref, turned_ref, names_ref, out_ref):
    total = sums_ref[0]
    rest = jnp.zeros((8, 128), F32)
    for k in range(1, N_SEP):
        total, lost = two_sum(total, sums_ref[k])
        rest = rest + lost
    rest = rest[0:1] + total[1:2]
    columns = [jnp.broadcast_to(line, (128, 128)).T[:, :1] for line in (total[0:1], rest)]
    rz, ru, qz, qu, zq, zw, uq, uw = [
        two_sum(*(column[k * COLS : (k + 1) * COLS] for column in columns)) for k in range(8)
    ]
    alpha = rz[0] / zq[0]
    newer = double_add(
        double_add(rz, double_scaled(double_add(ru, qz), -alpha)), double_scaled(double_scaled(qu, alpha), alpha)
    )[0]
    late_late = double_add(
        double_add(zq, double_scaled(double_add(zw, uq), -alpha)), double_scaled(double_scaled(uw, alpha), alpha)
    )[0]
    late_early = double_add(zq, double_scaled(uq, -alpha))[0]
    early_late = double_add(zq, double_scaled(zw, -alpha))[0]
    beta = newer / rz[0]
    energy = late_late + beta * (late_early + early_late) + beta * beta * zq[0]
    late = newer / energy
    search = search_ref[...]
    value = (alpha + late * beta) * search + late * (search - alpha * turned_ref[...])
    natural = lax.broadcasted_iota(jnp.int32, (1, ROWS), 1).astype(F32)
    rows = taken(value[:, :ROWS], places_of(names_ref[...], natural))
    for b in range(N_BLK):
        m = b % SETS
        out_ref[b, :, :HALF] = value[:, m * HALF : (m + 1) * HALF]
        out_ref[b, :, HALF : 2 * HALF] = value[:, ROWS + m * HALF : ROWS + (m + 1) * HALF]
        out_ref[b, :, 2 * HALF :] = rows[:, b * 128 : (b + 1) * 128]


def sort_kernel(early_ref, ports_ref, schur_ref, outer_ref, product_ref, keep_ref, send_ref, message_ref, low_order_ref, high_order_ref):
    row = lax.broadcasted_iota(jnp.int32, (HALF, HALF), 0)
    column = lax.broadcasted_iota(jnp.int32, (HALF, HALF), 1)
    reduced = outer_ref[...].T - product_ref[...]
    into, moved_sides = [], []
    for side, order_ref in ((0, low_order_ref), (1, high_order_ref)):
        at = slice(side * HALF, (side + 1) * HALF)
        names = ports_ref[:, at].astype(F32)
        across = jnp.broadcast_to(names, (HALF, HALF))
        rank = jnp.sum((across.T < across).astype(F32), axis=0, keepdims=True)
        order = (row.astype(F32) == rank).astype(F32)
        order_ref[...] = order.astype(BF16)
        into.append(order.T.astype(BF16))
        moved_sides.append(moved(jnp.concatenate([reduced[:, at], jnp.broadcast_to(names, (8, HALF))], axis=0), into[side]))
    lower = moved(moved(schur_ref[:HALF, :HALF], into[0]).T, into[0])
    higher = moved(moved(schur_ref[HALF:, HALF:], into[1]).T, into[1])
    across = moved(moved(schur_ref[HALF:, :HALF], into[0]).T, into[1])
    packed = jnp.where(row <= column, lower, higher)
    early = early_ref[0] == 1
    keep_ref[...] = jnp.where(early, across, packed)
    send_ref[...] = jnp.where(early, packed, across)
    extra_row = lax.broadcasted_iota(jnp.int32, (EXTRA, HALF), 0)
    for side, matrix in ((0, lower), (1, higher)):
        at = slice(side * HALF, (side + 1) * HALF)
        diagonal = jnp.sum(jnp.where(row == column, matrix, 0.0), axis=0, keepdims=True)
        names = moved_sides[side][128:]
        extra = jnp.where(extra_row == 0, diagonal, jnp.where(extra_row == 1, names, 0.0))
        for c in range(N_BLK):
            message_ref[c, :COLS, at] = moved_sides[side][c * COLS : (c + 1) * COLS]
            message_ref[c, COLS:, at] = extra


def split_kernel(value_ref, high_ref, low_ref):
    high_ref[...], low_ref[...] = split2(value_ref[...])


def interior_kernel(voltage_ref, low_order_ref, high_order_ref, high_ref, low_ref, inner_ref, interior_ref, port_ref):
    local = jnp.concatenate(
        [moved(voltage_ref[:, :HALF], low_order_ref[...]), moved(voltage_ref[:, HALF : 2 * HALF], high_order_ref[...])],
        axis=1,
    )
    high, low = split2(local)

    def turned(left, right):
        return lax.dot_general(left, right, (((1,), (1,)), ((), ())), preferred_element_type=F32)

    solved = high_ref[...]
    interior_ref[...] = inner_ref[...] - (turned(solved, high) + (turned(solved, low) + turned(low_ref[...], high)))
    port_ref[...] = voltage_ref[:, 2 * HALF :].T


def body(interior_inverse, coupling, port_matrix, interior_current, port_current, port_list, spectral_scale):
    ginv = interior_inverse[0, 0]
    aip = coupling[0, 0]
    app = port_matrix[0, 0]
    inner = interior_current[0, 0]
    outer = port_current[0, 0]
    ports = port_list[0, 0]
    b = lax.axis_index("blk")

    solved = jnp.dot(ginv, aip, precision=MID)
    schur = app - jnp.dot(aip.T, solved, precision=MID)
    product = jnp.dot(inner.T, solved, precision=MID)
    own_inner = jnp.dot(ginv, inner, precision=MID)

    square = ((HALF, HALF), F32)
    order = ((HALF, HALF), BF16)
    keep, send, message, low_order, high_order = kernel_call(
        sort_kernel,
        [square, square, ((N_BLK, COLS + EXTRA, 2 * HALF), F32), order, order],
        (b < SETS).astype(jnp.int32).reshape(1),
        ports.reshape(1, 2 * HALF),
        schur,
        outer,
        product,
        scalars=1,
    )
    solved_high, solved_low = kernel_call(split_kernel, [((NI, 2 * HALF), BF16)] * 2, solved)
    got = shifted(send, "blk", SETS, N_BLK)
    got, own_inner, solved_high, solved_low = lax.optimization_barrier((got, own_inner, solved_high, solved_low))
    mine = keep + got
    packs = [mine] + [shifted(mine, "blk", d, N_BLK) for d in (4, 2, 6)]
    sources = [b, (b - 2) % N_BLK, b ^ 1, ((b ^ 1) - 2) % N_BLK]

    parts = lax.all_to_all(message, "blk", 0, 0, tiled=True)
    sums = parts[:SETS] + parts[SETS:]
    by_rows = jnp.transpose(sums, (1, 0, 2))
    lower = by_rows[:, :, :HALF].reshape(COLS + EXTRA, ROWS)
    higher = by_rows[:, :, HALF:].reshape(COLS + EXTRA, ROWS)
    before = shifted(higher, "sep", 1, N_SEP)
    after = shifted(lower, "sep", -1, N_SEP)
    *packs, before, after = lax.optimization_barrier((*packs, before, after))
    packs = packs + [lax.ppermute(pack, "blk", [(i, i ^ 1) for i in range(N_BLK)]) for pack in packs]
    vec = ((COLS, 2 * ROWS), F32)
    line = ((1, 2 * ROWS), F32)
    side = ((COLS, ROWS), F32)
    choice = ((1, ROWS), jnp.int32)
    into_lower, into_higher, rhs, inverse, damped, level = kernel_call(
        initial_kernel, [choice, choice, vec, line, line, vec], spectral_scale.reshape(1), lower, higher, before, after, scalars=1
    )
    order = jnp.stack([source % SETS for source in sources] + [(source < SETS).astype(jnp.int32) for source in sources])
    *matrices, low, high = kernel_call(
        matrices_kernel,
        [((SETS, 2 * HALF, 2 * HALF), BF16)] * 2 + [side, side],
        order,
        *packs,
        sums[:, COLS : COLS + 1, HALF:],
        level,
        scalars=1,
    )

    def exchanged(low, high):
        return low, high, shifted(high, "sep", 1, N_SEP), shifted(low, "sep", -1, N_SEP)

    def applied(kernel, outs, low, high, *others):
        return kernel_call(kernel, outs, *matrices, into_lower, into_higher, *exchanged(low, high), *others)

    low, high, level, total = applied(middle_kernel, [side, side, vec, vec], low, high, damped, level)
    q_low, q_high, search = applied(last_kernel, [side, side, vec], low, high, damped, level, total)
    low, high, image, level = applied(image_kernel, [side, side, vec, vec], q_low, q_high, inverse)
    low, high, level, total = applied(middle_kernel, [side, side, vec, vec], low, high, damped, level)
    turned, products, _, _ = applied(
        closing_kernel,
        [vec, ((N_SEP, 8, 128), F32), side, side],
        low, high, damped, level, total, rhs, search, image, q_low, q_high,
    )
    products = lax.all_to_all(products, "sep", 0, 0, tiled=True)
    own_names = 0.5 * lower[COLS + 1 : COLS + 2]
    (spread,) = kernel_call(voltage_kernel, [((N_BLK, COLS, 640), F32)], products, search, turned, own_names)
    voltage = lax.all_to_all(spread, "blk", 0, 0, tiled=True).reshape(128, 640)
    interior, port = kernel_call(
        interior_kernel, [((NI, 128), F32), ((128, 128), F32)], voltage, low_order, high_order, solved_high, solved_low, own_inner
    )
    return port[None], interior[None, None]


def solution(mesh):
    return jax.shard_map(
        body,
        mesh=mesh,
        in_specs=(
            P("blk", "sep", None, None),
            P("blk", "sep", None, None),
            P("blk", "sep", None, None),
            P("blk", "sep", None, None),
            P("blk", "sep", None, None),
            P("blk", "sep", None),
            P(),
        ),
        out_specs=(P("sep", "blk", None), P("blk", "sep", None, None)),
        check_vma=False,
    )
```
